512 devices in a mesh: dp: 32 (over z, y_hi), expert: 16 (over y_lo, x, core).
Axes of the slice: x: 4, y: 4 (y_hi: 2, y_lo: 2; y = y_hi * 2 + y_lo), z: 16, core: 2. Of those that a mesh axis runs over, the one named last changes fastest.
Arguments:
- weight: bfloat16 [16, 1024, 4096], P('expert', None, 'dp'), may hold values from -0.1875 to 0.1875
- first_moment: float32 [16, 1024, 4096], P('expert', None, 'dp'), may hold values from -3 to 3
- second_moment: float32 [16, 1024, 4096], P('expert', None, 'dp'), may hold values from 0.01 to 1
- gate_act: bfloat16 [16, 4096, 1024], P('expert', 'dp'), may hold values from -6 to 6
- up_act: bfloat16 [16, 4096, 1024], P('expert', 'dp'), may hold values from -6 to 6
- out_grad: bfloat16 [16, 4096, 4096], P('expert', 'dp'), may hold values from -0.29882812 to 0.29882812
- old_host: int32 [16], replicated, may hold values from 0 to 15, each once
- new_host: int32 [16], replicated, may hold values from 0 to 15, each once
- counts: int32 [32, 16], replicated, may hold values from 1 to 128, as said below
Outputs:
- expert_out: bfloat16 [16, 4096, 4096], P('expert', 'dp')
- new_weight: bfloat16 [16, 1024, 4096], P('expert', None, 'dp')
- new_first: float32 [16, 1024, 4096], P('expert', None, 'dp')
- new_second: float32 [16, 1024, 4096], P('expert', None, 'dp')
The draws below stay inside these ranges and needn't reach their ends.
Inputs may be any that keep to these rules, and one draw needn't show every extreme that they name: `old_host`: each expert's host index appears once. `new_host`: each expert's host index appears once. `counts`: some expert from some replica fills all 128 slots.
All inputs are finite; a program needn't handle non-finite values.
Results may differ from the reference program's by a relative error of at most 0.0049.
Values may be sent and summed in bfloat16 or wider, within the bound.
No kernel may reach another device: no remote copies, remote signals or barrier semaphores. Data moves between devices by JAX's collectives and lax.ppermute only.
A program may use at most 64 MiB of HBM per device.

```python
import math
import jax
import jax.numpy as jnp
from jax import lax

D = 4096
FF = 1024
CAP = 128
EXPERTS = 16
ROWS_ALL = 4096
N_DP = 32


def draw_counts(key, part):
    key_level, key_count, key_row, key_col = jax.random.split(key, 4)
    levels = jax.random.randint(key_level, (EXPERTS,), 1, 5)
    upper = CAP * levels // 4
    lower = jnp.maximum(upper // 2, 1)
    raw_draw = jax.random.randint(key_count, (N_DP, EXPERTS), 0, 1 << 20)
    drawn = lower[None, :] + raw_draw % (upper - lower + 1)[None, :]
    full_row = jax.random.randint(key_row, (), 0, N_DP)
    full_col = jax.random.randint(key_col, (), 0, EXPERTS)
    return drawn.at[full_row, full_col].set(CAP).astype(jnp.int32)


def shard_levels(rng, shape, pieces, low, top_value):
    loudness, own = 1.0, jax.random.fold_in(rng, 6)
    for axis_at, blocks in pieces:
        heights = jnp.exp(jax.random.uniform(jax.random.fold_in(own, axis_at), (blocks,), jnp.float32, low / len(pieces), top_value / len(pieces)))
        loudness = loudness * jnp.repeat(heights, shape[axis_at] // blocks).reshape([-1 if axis == axis_at else 1 for axis in range(len(shape))])
    return loudness


def bell_draw(rng, extent, width, reach, cuts=(), kind=jnp.bfloat16):
    values = jax.random.normal(rng, extent, jnp.float32) * width
    if len(cuts) > 0:
        values = shard_levels(rng, extent, cuts, -0.22, 0.18) * values
    return jnp.clip(values, min=-reach, max=reach).astype(kind)


def setup_inputs(seed: int = 0) -> dict:
    key_list = jax.random.split(jax.random.key(seed), 10)
    return {
        "weight": bell_draw(key_list[0], (EXPERTS, FF, D), FF ** -0.5, 0.1875, ((0, 16), (2, 32))),
        "first_moment": bell_draw(key_list[1], (EXPERTS, FF, D), 0.5, 3.0, ((0, 16), (2, 32)), jnp.float32),
        "second_moment": jnp.clip(jnp.exp(math.log(1.0) - 4.6051702 * jax.random.uniform(key_list[2], (EXPERTS, FF, D), jnp.float32) ** shard_levels(key_list[2], (EXPERTS, FF, D), ((0, 16), (2, 32)), -0.2, 0.2)), 0.01, 1.0),
        "gate_act": bell_draw(key_list[3], (EXPERTS, ROWS_ALL, FF), 1.0, 6.0, ((0, 16), (1, 32))),
        "up_act": bell_draw(key_list[4], (EXPERTS, ROWS_ALL, FF), 1.0, 6.0, ((0, 16), (1, 32))),
        "out_grad": bell_draw(key_list[5], (EXPERTS, ROWS_ALL, D), 0.05, 0.29882812, ((0, 16), (1, 32))),
        "old_host": jax.random.permutation(key_list[6], EXPERTS).astype(jnp.int32),
        "new_host": jax.random.permutation(key_list[7], EXPERTS).astype(jnp.int32),
        "counts": draw_counts(jax.random.fold_in(key_list[9], 71), 0),
    }


beta_one = 0.9
beta_two = 0.999
learning_rate = 0.001
epsilon_value = 1e-08
bias_one = 0.9999734386011124
bias_two = 0.0952078528863

def reference(weight, first_moment, second_moment, gate_act, up_act, out_grad, old_host, new_host, counts):
    host_ids = jnp.arange(EXPERTS, dtype=jnp.int32)
    expert_of = jnp.zeros((EXPERTS,), jnp.int32).at[new_host].set(host_ids)
    row_ids = jnp.arange(CAP * N_DP, dtype=jnp.int32)
    replica_of = row_ids // CAP
    slot_of = row_ids % CAP

    def per_host(host_id):
        expert_id = expert_of[host_id]
        source = old_host[expert_id]
        moved_weight = weight[source]
        moved_first = first_moment[source]
        moved_second = second_moment[source]
        live_rows = counts[:, expert_id]
        filled = slot_of < live_rows[replica_of]
        gate_value = gate_act[host_id].astype(jnp.float32)
        up_value = up_act[host_id].astype(jnp.float32)
        hidden = jnp.where(filled[:, None], jax.nn.silu(gate_value) * up_value, jnp.float32(0.0)).astype(jnp.bfloat16)
        output = jnp.dot(hidden, moved_weight, preferred_element_type=jnp.float32).astype(jnp.bfloat16)
        grad = jnp.dot(hidden.T, out_grad[host_id], preferred_element_type=jnp.float32)
        new_first = beta_one * moved_first + (1.0 - beta_one) * grad
        new_second = beta_two * moved_second + (1.0 - beta_two) * grad * grad
        update = learning_rate * (new_first / bias_one) / (jnp.sqrt(new_second / bias_two) + epsilon_value)
        new_weight = (moved_weight.astype(jnp.float32) - update).astype(jnp.bfloat16)
        return (output, new_weight, new_first, new_second)
    expert_out, new_weight, new_first, new_second = lax.map(per_host, host_ids)
    return (expert_out, new_weight, new_first, new_second)
```

```python
import functools

import jax
import jax.numpy as jnp
from jax import lax
from jax.experimental import pallas as pl
from jax.experimental.pallas import tpu as pltpu
from jax.sharding import Mesh, PartitionSpec as P

beta_one = 0.9
beta_two = 0.999
learning_rate = 0.001
epsilon_value = 1e-08
bias_one = 0.9999734386011124
bias_two = 0.0952078528863

N_FAR = 8
N_Z = 16
TEAM = ("near", "half")
SWAP = [(0, 1), (1, 0)]
UP = [(i, (i + 1) % N_FAR) for i in range(N_FAR)]
DOWN = [(i, (i - 1) % N_FAR) for i in range(N_FAR)]
VMEM = pl.BlockSpec(memory_space=pltpu.VMEM)
SMEM = pl.BlockSpec(memory_space=pltpu.SMEM)
ANY = pl.BlockSpec(memory_space=pl.ANY)
FIRST = [4, 3, -3]
SECOND = [2, -2, 1, -1, 0]


def shape(dims, dtype=jnp.bfloat16):
    return jax.ShapeDtypeStruct(dims, dtype)


def cost(flops, moved):
    return pl.CostEstimate(flops=flops, bytes_accessed=moved, transcendentals=0)


def prepare_kernel(place, new_host, counts, gate, up, cotangent, one, two):
    ring, member, host = place[0], place[1], place[2]
    expert = jnp.int32(0)
    for k in range(new_host.shape[0]):
        expert = jnp.where(new_host[k] == host, k, expert)
    live = counts[ring * 4 + member, expert]
    value = gate[...].astype(jnp.float32)
    activated = value / (1.0 + jnp.exp(-value)) * up[...].astype(jnp.float32)
    slot = lax.broadcasted_iota(jnp.int32, activated.shape, 0)
    hidden = jnp.where(slot < live, activated, 0.0).astype(one.dtype)
    for mate in range(4):
        for k in range(hidden.shape[1] // 128):
            one[mate, len(FIRST) + k] = hidden[:, k * 128 : (k + 1) * 128]
    for group, blocks in ((FIRST, one), (SECOND, two)):
        for i, distance in enumerate(group):
            owner = lax.rem(ring + (distance + N_FAR), N_FAR) * 4
            for mate in range(4):
                start = pl.multiple_of((owner + mate) * 128, 128)
                blocks[mate, i] = cotangent[:, pl.ds(start, 128)]


def prepare(place, new_host, counts, gate, up, cotangent):
    return pl.pallas_call(
        prepare_kernel,
        out_shape=[
            shape((4, len(FIRST) + gate.shape[1] // 128, gate.shape[0], 128)),
            shape((4, len(SECOND), gate.shape[0], 128)),
        ],
        in_specs=[SMEM] * 3 + [VMEM] * 3,
        out_specs=[VMEM] * 2,
        cost_estimate=cost(0, 3 << 20),
        name="prepare",
    )(place, new_host, counts, gate, up, cotangent)


def part_of(blocks, i, rows):
    block = jnp.concatenate([blocks[mate, i] for mate in range(4)], axis=0)
    total = lax.dot_general(
        block, rows[...], (((0,), (0,)), ((), ())), preferred_element_type=jnp.float32
    )
    return total.astype(rows.dtype)


def first_kernel(blocks, after, rows, low, high, *out):
    size = blocks.shape[2]
    for mate in range(4):
        for k in range(blocks.shape[1] - len(FIRST)):
            rows[pl.ds(mate * size, size), pl.ds(k * 128, 128)] = blocks[mate, len(FIRST) + k]
    total = part_of(blocks, 0, rows)
    half = total.shape[0] // 2
    low[...] = total[:half]
    high[...] = total[half:]
    for i, ref in enumerate(out):
        ref[...] = part_of(blocks, i + 1, rows)


def first_parts(blocks, after):
    columns, hidden_units = blocks.shape[3], (blocks.shape[1] - len(FIRST)) * 128
    return pl.pallas_call(
        first_kernel,
        out_shape=[shape((4 * blocks.shape[2], hidden_units))]
        + [shape((columns // 2, hidden_units))] * 2
        + [shape((columns, hidden_units))] * (len(FIRST) - 1),
        in_specs=[VMEM, ANY],
        out_specs=[VMEM] * (len(FIRST) + 2),
        cost_estimate=cost(1 << 28, 3 << 20),
        name="first_parts",
    )(blocks, after)


def second_kernel(blocks, rows, *out):
    for i, ref in enumerate(out):
        ref[...] = part_of(blocks, i, rows)


def second_parts(blocks, rows):
    return pl.pallas_call(
        second_kernel,
        out_shape=[shape((blocks.shape[3], rows.shape[1]))] * len(SECOND),
        in_specs=[VMEM] * 2,
        out_specs=[VMEM] * len(SECOND),
        cost_estimate=cost(1 << 29, 3 << 20),
        name="second_parts",
    )(blocks, rows)


def produce_kernel(mate, place, rows, blocks, out):
    member = place[1]
    if mate:
        member = member + 1 - 2 * lax.rem(member, 2)
    size = out.shape[1]
    mine = rows[pl.ds(pl.multiple_of(member * size, size), size), :]
    for i in range(blocks.shape[0]):
        out[i] = jnp.dot(mine, blocks[i], preferred_element_type=jnp.float32).astype(out.dtype)


def produce(mate, place, rows, blocks):
    count, hidden_units, columns = blocks.shape
    size, step = rows.shape[0] // 4, 4
    return pl.pallas_call(
        functools.partial(produce_kernel, mate),
        out_shape=shape((count, size, columns)),
        grid=(count // step,),
        in_specs=[
            SMEM,
            pl.BlockSpec(rows.shape, lambda i: (0, 0)),
            pl.BlockSpec((step, hidden_units, columns), lambda i: (i, 0, 0)),
        ],
        out_specs=pl.BlockSpec((step, size, columns), lambda i: (i, 0, 0)),
        cost_estimate=cost(count << 25, 5 << 20),
        name="produce",
    )(place, rows, blocks)


def reorder_kernel(old_host, new_host, value, *refs):
    out = refs[-1]
    for k in range(value.shape[0]):
        out[new_host[k]] = value[old_host[k]]


def reorder(value, old_host, new_host, after):
    return pl.pallas_call(
        reorder_kernel,
        out_shape=shape(value.shape, value.dtype),
        in_specs=[SMEM] * 2 + [VMEM] + [ANY] * len(after),
        out_specs=VMEM,
        cost_estimate=cost(0, 2 * value.size * value.dtype.itemsize),
        name="reorder",
    )(old_host, new_host, value, *after)


def relocate(blocks, old_host, new_host, *after):
    spread = lax.all_to_all(blocks, "expert", split_axis=0, concat_axis=0, tiled=True)
    ordered = reorder(spread, old_host, new_host, after)
    return lax.all_to_all(ordered, "expert", split_axis=0, concat_axis=0, tiled=True)


def assemble_kernel(place, near, far, out):
    half = lax.rem(place[1], 2)
    for owner in range(N_Z):
        for side, ref in ((half, near), (1 - half, far)):
            start = pl.multiple_of((2 * owner + side) * 128, 128)
            out[:, pl.ds(start, 128)] = ref[owner]


def assemble(place, near, far):
    return pl.pallas_call(
        assemble_kernel,
        out_shape=shape((near.shape[1], 2 * N_Z * 128)),
        in_specs=[SMEM] + [VMEM] * 2,
        out_specs=VMEM,
        cost_estimate=cost(0, 2 << 20),
        name="assemble",
    )(place, near, far)


def adam_kernel(weight, moments, part, rising, falling, new_weight, new_first, new_second):
    hosts, both, _ = moments.shape
    step = both // 2
    grad = part[...].astype(jnp.float32) + rising[...].astype(jnp.float32)
    grad = (grad + falling[...].astype(jnp.float32)).T
    for d in range(hosts):
        at = pl.ds(d * step, step)
        g = grad[d * step : (d + 1) * step]
        first = beta_one * moments[d, :step] + (1.0 - beta_one) * g
        second = beta_two * moments[d, step:] + (1.0 - beta_two) * g * g
        update = (
            learning_rate * (first / bias_one) / (jnp.sqrt(second / bias_two) + epsilon_value)
        )
        new_first[at] = first
        new_second[at] = second
        new_weight[at] = (weight[at].astype(jnp.float32) - update).astype(new_weight.dtype)


def adam(weight, moments, part, rising, falling):
    return pl.pallas_call(
        adam_kernel,
        out_shape=[
            shape(weight.shape),
            shape(weight.shape, jnp.float32),
            shape(weight.shape, jnp.float32),
        ],
        in_specs=[VMEM] * 5,
        out_specs=[VMEM] * 3,
        cost_estimate=cost(0, 3 << 20),
        name="adam",
    )(weight, moments, part, rising, falling)


def add(left, right):
    return (left.astype(jnp.float32) + right.astype(jnp.float32)).astype(jnp.bfloat16)


def local(
    weight, first_moment, second_moment, gate_act, up_act, out_grad, old_host, new_host, counts
):
    hosts = lax.axis_size("expert")
    ring, member = lax.axis_index("ring"), lax.axis_index(TEAM)
    at = jnp.arange(3, dtype=jnp.int32)
    place = jnp.where(at == 0, ring, jnp.where(at == 1, member, lax.axis_index("expert")))
    hidden_units, columns = weight.shape[1:]
    block_rows = hidden_units // hosts
    half = columns // 2

    one, two = prepare(place, new_host, counts, gate_act[0], up_act[0], out_grad[0])
    one = lax.all_to_all(one, TEAM, split_axis=0, concat_axis=0, tiled=True)
    two = lax.all_to_all(two, TEAM, split_axis=0, concat_axis=0, tiled=True)
    spread = lax.all_to_all(
        weight.reshape(hosts, block_rows, columns), "expert", split_axis=0, concat_axis=0, tiled=True
    )
    ordered = reorder(spread, old_host, new_host, [])
    moved_weight = lax.all_to_all(ordered, "expert", split_axis=0, concat_axis=0, tiled=True)
    moved_weight = moved_weight.reshape(hidden_units, columns)
    rows, low, high, *part = first_parts(one, ordered)
    part = dict(zip(FIRST[1:] + SECOND, [*part, *second_parts(two, rows)]))

    gathered = lax.all_gather(moved_weight, ("ring", "near"), axis=0, tiled=False)
    far = lax.ppermute(produce(True, place, rows, gathered), "half", SWAP)
    output = assemble(place, produce(False, place, rows, gathered), far)

    up_sum, down_sum = low, high
    for step in range(1, N_FAR // 2 + 1):
        up_sum = lax.ppermute(up_sum, "ring", UP)
        down_sum = lax.ppermute(down_sum, "ring", DOWN)
        if step < N_FAR // 2:
            up_part, down_part = part[N_FAR // 2 - step], part[step - N_FAR // 2]
            if step == 1:
                up_sum = jnp.concatenate([add(up_sum, up_part[:half]), up_part[half:]])
                down_sum = jnp.concatenate([down_part[:half], add(down_sum, down_part[half:])])
            else:
                up_sum, down_sum = add(up_sum, up_part), add(down_sum, down_part)
        if step == 1:
            stacked = jnp.concatenate(
                [
                    first_moment.reshape(hosts, block_rows, columns),
                    second_moment.reshape(hosts, block_rows, columns),
                ],
                axis=1,
            )
            stacked, up_sum = lax.optimization_barrier((stacked, up_sum))
            moments = relocate(stacked, old_host, new_host)
        if step == 3:
            up_sum, moments = lax.optimization_barrier((up_sum, moments))
    new_weight, new_first, new_second = adam(moved_weight, moments, part[0], up_sum, down_sum)
    return (output[None], new_weight[None], new_first[None], new_second[None])


def solution(mesh):
    hosts = mesh.shape["expert"]
    grid = Mesh(mesh.devices.reshape(N_FAR, 2, 2, hosts), ("ring", "near", "half", "expert"))
    shards = P("expert", None, ("ring", "near", "half"))
    tokens = P("expert", ("ring", "near", "half"), None)
    return jax.shard_map(
        local,
        mesh=grid,
        in_specs=(shards, shards, shards, tokens, tokens, tokens, P(), P(), P()),
        out_specs=(tokens, shards, shards, shards),
        check_vma=False,
    )
```

```python
import functools

import jax
import jax.numpy as jnp
from jax import lax
from jax.experimental import pallas as pl
from jax.experimental.pallas import tpu as pltpu
from jax.sharding import Mesh, PartitionSpec as P

beta_one = 0.9
beta_two = 0.999
learning_rate = 0.001
epsilon_value = 1e-08
bias_one = 0.9999734386011124
bias_two = 0.0952078528863

N_FAR = 8
N_Z = 16
TEAM = ("near", "half")
SWAP = [(0, 1), (1, 0)]
UP = [(i, (i + 1) % N_FAR) for i in range(N_FAR)]
DOWN = [(i, (i - 1) % N_FAR) for i in range(N_FAR)]
VMEM = pl.BlockSpec(memory_space=pltpu.VMEM)
SMEM = pl.BlockSpec(memory_space=pltpu.SMEM)
ANY = pl.BlockSpec(memory_space=pl.ANY)
FIRST = [4, 3, -3]
SECOND = [2, -2, 1, -1, 0]


def shape(dims, dtype=jnp.bfloat16):
    return jax.ShapeDtypeStruct(dims, dtype)


def cost(flops, moved):
    return pl.CostEstimate(flops=flops, bytes_accessed=moved, transcendentals=0)


def prepare_kernel(place, new_host, counts, gate, up, cotangent, one, two):
    ring, member, host = place[0], place[1], place[2]
    expert = jnp.int32(0)
    for k in range(new_host.shape[0]):
        expert = jnp.where(new_host[k] == host, k, expert)
    live = counts[ring * 4 + member, expert]
    value = gate[...].astype(jnp.float32)
    activated = value / (1.0 + jnp.exp(-value)) * up[...].astype(jnp.float32)
    slot = lax.broadcasted_iota(jnp.int32, activated.shape, 0)
    hidden = jnp.where(slot < live, activated, 0.0).astype(one.dtype)
    for mate in range(4):
        for k in range(hidden.shape[1] // 128):
            one[mate, len(FIRST) + k] = hidden[:, k * 128 : (k + 1) * 128]
    for group, blocks in ((FIRST, one), (SECOND, two)):
        for i, distance in enumerate(group):
            owner = lax.rem(ring + (distance + N_FAR), N_FAR) * 4
            for mate in range(4):
                start = pl.multiple_of((owner + mate) * 128, 128)
                blocks[mate, i] = cotangent[:, pl.ds(start, 128)]


def prepare(place, new_host, counts, gate, up, cotangent):
    return pl.pallas_call(
        prepare_kernel,
        out_shape=[
            shape((4, len(FIRST) + gate.shape[1] // 128, gate.shape[0], 128)),
            shape((4, len(SECOND), gate.shape[0], 128)),
        ],
        in_specs=[SMEM] * 3 + [VMEM] * 3,
        out_specs=[VMEM] * 2,
        cost_estimate=cost(0, 3 << 20),
        name="prepare",
    )(place, new_host, counts, gate, up, cotangent)


def part_of(blocks, i, rows):
    block = jnp.concatenate([blocks[mate, i] for mate in range(4)], axis=0)
    total = lax.dot_general(
        block, rows[...], (((0,), (0,)), ((), ())), preferred_element_type=jnp.float32
    )
    return total.astype(rows.dtype)


def first_kernel(blocks, after, rows, low, high, *out):
    size = blocks.shape[2]
    for mate in range(4):
        for k in range(blocks.shape[1] - len(FIRST)):
            rows[pl.ds(mate * size, size), pl.ds(k * 128, 128)] = blocks[mate, len(FIRST) + k]
    total = part_of(blocks, 0, rows)
    half = total.shape[0] // 2
    low[...] = total[:half]
    high[...] = total[half:]
    for i, ref in enumerate(out):
        ref[...] = part_of(blocks, i + 1, rows)


def first_parts(blocks, after):
    columns, hidden_units = blocks.shape[3], (blocks.shape[1] - len(FIRST)) * 128
    return pl.pallas_call(
        first_kernel,
        out_shape=[shape((4 * blocks.shape[2], hidden_units))]
        + [shape((columns // 2, hidden_units))] * 2
        + [shape((columns, hidden_units))] * (len(FIRST) - 1),
        in_specs=[VMEM, ANY],
        out_specs=[VMEM] * (len(FIRST) + 2),
        cost_estimate=cost(1 << 28, 3 << 20),
        name="first_parts",
    )(blocks, after)


def second_kernel(blocks, rows, *out):
    for i, ref in enumerate(out):
        ref[...] = part_of(blocks, i, rows)


def second_parts(blocks, rows):
    return pl.pallas_call(
        second_kernel,
        out_shape=[shape((blocks.shape[3], rows.shape[1]))] * len(SECOND),
        in_specs=[VMEM] * 2,
        out_specs=[VMEM] * len(SECOND),
        cost_estimate=cost(1 << 29, 3 << 20),
        name="second_parts",
    )(blocks, rows)


def produce_kernel(mate, place, rows, blocks, *refs):
    out = refs[-1]
    member = place[1]
    if mate:
        member = member + 1 - 2 * lax.rem(member, 2)
    size = out.shape[1]
    mine = rows[pl.ds(pl.multiple_of(member * size, size), size), :]
    for i in range(blocks.shape[0]):
        out[i] = jnp.dot(mine, blocks[i], preferred_element_type=jnp.float32).astype(out.dtype)


def produce(mate, place, rows, blocks, after):
    count, hidden_units, columns = blocks.shape
    size, step = rows.shape[0] // 4, 4
    return pl.pallas_call(
        functools.partial(produce_kernel, mate),
        out_shape=shape((count, size, columns)),
        grid=(count // step,),
        in_specs=[
            SMEM,
            pl.BlockSpec(rows.shape, lambda i: (0, 0)),
            pl.BlockSpec((step, hidden_units, columns), lambda i: (i, 0, 0)),
        ]
        + [ANY] * len(after),
        out_specs=pl.BlockSpec((step, size, columns), lambda i: (i, 0, 0)),
        cost_estimate=cost(count << 25, 5 << 20),
        name="produce",
    )(place, rows, blocks, *after)


def reorder_kernel(old_host, new_host, value, *refs):
    out = refs[-1]
    for k in range(value.shape[0]):
        out[new_host[k]] = value[old_host[k]]


def reorder(value, old_host, new_host, after):
    return pl.pallas_call(
        reorder_kernel,
        out_shape=shape(value.shape, value.dtype),
        in_specs=[SMEM] * 2 + [VMEM] + [ANY] * len(after),
        out_specs=VMEM,
        cost_estimate=cost(0, 2 * value.size * value.dtype.itemsize),
        name="reorder",
    )(old_host, new_host, value, *after)


def assemble_kernel(place, near, far, out):
    half = lax.rem(place[1], 2)
    for owner in range(N_Z):
        for side, ref in ((half, near), (1 - half, far)):
            start = pl.multiple_of((2 * owner + side) * 128, 128)
            out[:, pl.ds(start, 128)] = ref[owner]


def assemble(place, near, far):
    return pl.pallas_call(
        assemble_kernel,
        out_shape=shape((near.shape[1], 2 * N_Z * 128)),
        in_specs=[SMEM] + [VMEM] * 2,
        out_specs=VMEM,
        cost_estimate=cost(0, 2 << 20),
        name="assemble",
    )(place, near, far)


def adam_kernel(weight, moments, part, rising, falling, after, new_weight, new_first, new_second):
    hosts, both, _ = moments.shape
    step = both // 2
    grad = part[...].astype(jnp.float32) + rising[...].astype(jnp.float32)
    grad = (grad + falling[...].astype(jnp.float32)).T
    for d in range(hosts):
        at = pl.ds(d * step, step)
        g = grad[d * step : (d + 1) * step]
        first = beta_one * moments[d, :step] + (1.0 - beta_one) * g
        second = beta_two * moments[d, step:] + (1.0 - beta_two) * g * g
        update = (
            learning_rate * (first / bias_one) / (jnp.sqrt(second / bias_two) + epsilon_value)
        )
        new_first[at] = first
        new_second[at] = second
        new_weight[at] = (weight[at].astype(jnp.float32) - update).astype(new_weight.dtype)


def adam(weight, moments, part, rising, falling, after):
    return pl.pallas_call(
        adam_kernel,
        out_shape=[
            shape(weight.shape),
            shape(weight.shape, jnp.float32),
            shape(weight.shape, jnp.float32),
        ],
        in_specs=[VMEM] * 5 + [ANY],
        out_specs=[VMEM] * 3,
        cost_estimate=cost(0, 3 << 20),
        name="adam",
    )(weight, moments, part, rising, falling, after)


def add(left, right):
    return (left.astype(jnp.float32) + right.astype(jnp.float32)).astype(jnp.bfloat16)


def local(
    weight, first_moment, second_moment, gate_act, up_act, out_grad, old_host, new_host, counts
):
    hosts = lax.axis_size("expert")
    ring, member = lax.axis_index("ring"), lax.axis_index(TEAM)
    at = jnp.arange(3, dtype=jnp.int32)
    place = jnp.where(at == 0, ring, jnp.where(at == 1, member, lax.axis_index("expert")))
    hidden_units, columns = weight.shape[1:]
    block_rows = hidden_units // hosts
    half = columns // 2

    one, two = prepare(place, new_host, counts, gate_act[0], up_act[0], out_grad[0])
    order = two
    one = lax.all_to_all(one, TEAM, split_axis=0, concat_axis=0, tiled=True)
    two = lax.all_to_all(two, TEAM, split_axis=0, concat_axis=0, tiled=True)
    spread = lax.all_to_all(
        weight.reshape(hosts, block_rows, columns), "expert", split_axis=0, concat_axis=0, tiled=True
    )
    ordered = reorder(spread, old_host, new_host, [order])
    moved_weight = lax.all_to_all(ordered, "expert", split_axis=0, concat_axis=0, tiled=True)
    moved_weight = moved_weight.reshape(hidden_units, columns)
    rows, low, high, *part = first_parts(one, order)
    part = dict(zip(FIRST[1:] + SECOND, [*part, *second_parts(two, rows)]))

    gathered = lax.all_gather(moved_weight, ("ring", "near"), axis=0, tiled=False)
    up_sum, down_sum = low, high
    stacked = jnp.concatenate(
        [
            first_moment.reshape(hosts, block_rows, columns),
            second_moment.reshape(hosts, block_rows, columns),
        ],
        axis=1,
    )
    stacked, part[0] = lax.optimization_barrier((stacked, part[0]))
    spread = lax.all_to_all(stacked, "expert", split_axis=0, concat_axis=0, tiled=True)
    ordered = reorder(spread, old_host, new_host, [])
    moments = lax.all_to_all(ordered, "expert", split_axis=0, concat_axis=0, tiled=True)
    for step in range(1, N_FAR // 2 + 1):
        last = [up_sum, down_sum]
        up_sum = lax.ppermute(up_sum, "ring", UP)
        down_sum = lax.ppermute(down_sum, "ring", DOWN)
        if step < N_FAR // 2:
            up_part, down_part = part[N_FAR // 2 - step], part[step - N_FAR // 2]
            if step == 1:
                up_sum = jnp.concatenate([add(up_sum, up_part[:half]), up_part[half:]])
                down_sum = jnp.concatenate([down_part[:half], add(down_sum, down_part[half:])])
            else:
                up_sum, down_sum = add(up_sum, up_part), add(down_sum, down_part)
    far = lax.ppermute(produce(True, place, rows, gathered, last), "half", SWAP)
    near = produce(False, place, rows, gathered, [])
    output = assemble(place, near, far)
    new_weight, new_first, new_second = adam(moved_weight, moments, part[0], up_sum, down_sum, near)
    return (output[None], new_weight[None], new_first[None], new_second[None])


def solution(mesh):
    hosts = mesh.shape["expert"]
    grid = Mesh(mesh.devices.reshape(N_FAR, 2, 2, hosts), ("ring", "near", "half", "expert"))
    shards = P("expert", None, ("ring", "near", "half"))
    tokens = P("expert", ("ring", "near", "half"), None)
    return jax.shard_map(
        local,
        mesh=grid,
        in_specs=(shards, shards, shards, tokens, tokens, tokens, P(), P(), P()),
        out_specs=(tokens, shards, shards, shards),
        check_vma=False,
    )
```

```python
import functools

import jax
import jax.numpy as jnp
from jax import lax
from jax.experimental import pallas as pl
from jax.experimental.pallas import tpu as pltpu
from jax.sharding import Mesh, PartitionSpec as P

beta_one = 0.9
beta_two = 0.999
learning_rate = 0.001
epsilon_value = 1e-08
bias_one = 0.9999734386011124
bias_two = 0.0952078528863

N_FAR = 8
N_Z = 16
TEAM = ("near", "half")
SWAP = [(0, 1), (1, 0)]
UP = [(i, (i + 1) % N_FAR) for i in range(N_FAR)]
DOWN = [(i, (i - 1) % N_FAR) for i in range(N_FAR)]
VMEM = pl.BlockSpec(memory_space=pltpu.VMEM)
SMEM = pl.BlockSpec(memory_space=pltpu.SMEM)
ANY = pl.BlockSpec(memory_space=pl.ANY)
FIRST = [4, 3, -3]
SECOND = [2, -2, 1, -1, 0]


def shape(dims, dtype=jnp.bfloat16):
    return jax.ShapeDtypeStruct(dims, dtype)


def cost(flops, moved):
    return pl.CostEstimate(flops=flops, bytes_accessed=moved, transcendentals=0)


def prepare_kernel(place, new_host, counts, gate, up, cotangent, one, two):
    ring, member, host = place[0], place[1], place[2]
    expert = jnp.int32(0)
    for k in range(new_host.shape[0]):
        expert = jnp.where(new_host[k] == host, k, expert)
    live = counts[ring * 4 + member, expert]
    value = gate[...].astype(jnp.float32)
    activated = value / (1.0 + jnp.exp(-value)) * up[...].astype(jnp.float32)
    slot = lax.broadcasted_iota(jnp.int32, activated.shape, 0)
    hidden = jnp.where(slot < live, activated, 0.0).astype(one.dtype)
    for mate in range(4):
        for k in range(hidden.shape[1] // 128):
            one[mate, len(FIRST) + k] = hidden[:, k * 128 : (k + 1) * 128]
    for group, blocks in ((FIRST, one), (SECOND, two)):
        for i, distance in enumerate(group):
            owner = lax.rem(ring + (distance + N_FAR), N_FAR) * 4
            for mate in range(4):
                start = pl.multiple_of((owner + mate) * 128, 128)
                blocks[mate, i] = cotangent[:, pl.ds(start, 128)]


def prepare(place, new_host, counts, gate, up, cotangent):
    return pl.pallas_call(
        prepare_kernel,
        out_shape=[
            shape((4, len(FIRST) + gate.shape[1] // 128, gate.shape[0], 128)),
            shape((4, len(SECOND), gate.shape[0], 128)),
        ],
        in_specs=[SMEM] * 3 + [VMEM] * 3,
        out_specs=[VMEM] * 2,
        cost_estimate=cost(0, 3 << 20),
        name="prepare",
    )(place, new_host, counts, gate, up, cotangent)


def part_of(blocks, i, rows):
    block = jnp.concatenate([blocks[mate, i] for mate in range(4)], axis=0)
    total = lax.dot_general(
        block, rows[...], (((0,), (0,)), ((), ())), preferred_element_type=jnp.float32
    )
    return total.astype(rows.dtype)


def first_kernel(blocks, after, rows, low, high, *out):
    size = blocks.shape[2]
    for mate in range(4):
        for k in range(blocks.shape[1] - len(FIRST)):
            rows[pl.ds(mate * size, size), pl.ds(k * 128, 128)] = blocks[mate, len(FIRST) + k]
    total = part_of(blocks, 0, rows)
    half = total.shape[0] // 2
    low[...] = total[:half]
    high[...] = total[half:]
    for i, ref in enumerate(out):
        ref[...] = part_of(blocks, i + 1, rows)


def first_parts(blocks, after):
    columns, hidden_units = blocks.shape[3], (blocks.shape[1] - len(FIRST)) * 128
    return pl.pallas_call(
        first_kernel,
        out_shape=[shape((4 * blocks.shape[2], hidden_units))]
        + [shape((columns // 2, hidden_units))] * 2
        + [shape((columns, hidden_units))] * (len(FIRST) - 1),
        in_specs=[VMEM, ANY],
        out_specs=[VMEM] * (len(FIRST) + 2),
        cost_estimate=cost(1 << 28, 3 << 20),
        name="first_parts",
    )(blocks, after)


def second_kernel(blocks, rows, *out):
    for i, ref in enumerate(out):
        ref[...] = part_of(blocks, i, rows)


def second_parts(blocks, rows):
    return pl.pallas_call(
        second_kernel,
        out_shape=[shape((blocks.shape[3], rows.shape[1]))] * len(SECOND),
        in_specs=[VMEM] * 2,
        out_specs=[VMEM] * len(SECOND),
        cost_estimate=cost(1 << 29, 3 << 20),
        name="second_parts",
    )(blocks, rows)


def produce_kernel(mate, place, rows, blocks, *refs):
    out = refs[-1]
    member = place[1]
    if mate:
        member = member + 1 - 2 * lax.rem(member, 2)
    size = out.shape[1]
    mine = rows[pl.ds(pl.multiple_of(member * size, size), size), :]
    columns = blocks.shape[2]
    for i in range(0, blocks.shape[0], 2):
        pair = jnp.concatenate([blocks[i], blocks[i + 1]], axis=1)
        total = jnp.dot(mine, pair, preferred_element_type=jnp.float32).astype(out.dtype)
        out[i] = total[:, :columns]
        out[i + 1] = total[:, columns:]


def produce(mate, place, rows, blocks, after):
    count, hidden_units, columns = blocks.shape
    size, step = rows.shape[0] // 4, 4
    return pl.pallas_call(
        functools.partial(produce_kernel, mate),
        out_shape=shape((count, size, columns)),
        grid=(count // step,),
        in_specs=[
            SMEM,
            pl.BlockSpec(rows.shape, lambda i: (0, 0)),
            pl.BlockSpec((step, hidden_units, columns), lambda i: (i, 0, 0)),
        ]
        + [ANY] * len(after),
        out_specs=pl.BlockSpec((step, size, columns), lambda i: (i, 0, 0)),
        cost_estimate=cost(count << 25, 5 << 20),
        name="produce",
    )(place, rows, blocks, *after)


def reorder_kernel(old_host, new_host, value, *refs):
    out = refs[-1]
    for k in range(value.shape[0]):
        out[new_host[k]] = value[old_host[k]]


def reorder(value, old_host, new_host, after):
    return pl.pallas_call(
        reorder_kernel,
        out_shape=shape(value.shape, value.dtype),
        in_specs=[SMEM] * 2 + [VMEM] + [ANY] * len(after),
        out_specs=VMEM,
        cost_estimate=cost(0, 2 * value.size * value.dtype.itemsize),
        name="reorder",
    )(old_host, new_host, value, *after)


def assemble_kernel(place, near, far, out):
    half = lax.rem(place[1], 2)
    for owner in range(N_Z):
        for side, ref in ((half, near), (1 - half, far)):
            start = pl.multiple_of((2 * owner + side) * 128, 128)
            out[:, pl.ds(start, 128)] = ref[owner]


def assemble(place, near, far):
    return pl.pallas_call(
        assemble_kernel,
        out_shape=shape((near.shape[1], 2 * N_Z * 128)),
        in_specs=[SMEM] + [VMEM] * 2,
        out_specs=VMEM,
        cost_estimate=cost(0, 2 << 20),
        name="assemble",
    )(place, near, far)


def adam_kernel(weight, moments, part, rising, falling, after, new_weight, new_first, new_second):
    hosts, both, _ = moments.shape
    step = both // 2
    grad = part[...].astype(jnp.float32) + rising[...].astype(jnp.float32)
    grad = (grad + falling[...].astype(jnp.float32)).T
    for d in range(hosts):
        at = pl.ds(d * step, step)
        g = grad[d * step : (d + 1) * step]
        first = beta_one * moments[d, :step] + (1.0 - beta_one) * g
        second = beta_two * moments[d, step:] + (1.0 - beta_two) * g * g
        update = (
            learning_rate * (first / bias_one) / (jnp.sqrt(second / bias_two) + epsilon_value)
        )
        new_first[at] = first
        new_second[at] = second
        new_weight[at] = (weight[at].astype(jnp.float32) - update).astype(new_weight.dtype)


def adam(weight, moments, part, rising, falling, after):
    return pl.pallas_call(
        adam_kernel,
        out_shape=[
            shape(weight.shape),
            shape(weight.shape, jnp.float32),
            shape(weight.shape, jnp.float32),
        ],
        in_specs=[VMEM] * 5 + [ANY],
        out_specs=[VMEM] * 3,
        cost_estimate=cost(0, 3 << 20),
        name="adam",
    )(weight, moments, part, rising, falling, after)


def add(left, right):
    return (left.astype(jnp.float32) + right.astype(jnp.float32)).astype(jnp.bfloat16)


def local(
    weight, first_moment, second_moment, gate_act, up_act, out_grad, old_host, new_host, counts
):
    hosts = lax.axis_size("expert")
    ring, member = lax.axis_index("ring"), lax.axis_index(TEAM)
    at = jnp.arange(3, dtype=jnp.int32)
    place = jnp.where(at == 0, ring, jnp.where(at == 1, member, lax.axis_index("expert")))
    hidden_units, columns = weight.shape[1:]
    block_rows = hidden_units // hosts
    half = columns // 2

    one, two = prepare(place, new_host, counts, gate_act[0], up_act[0], out_grad[0])
    order = two
    one = lax.all_to_all(one, TEAM, split_axis=0, concat_axis=0, tiled=True)
    two = lax.all_to_all(two, TEAM, split_axis=0, concat_axis=0, tiled=True)
    spread = lax.all_to_all(
        weight.reshape(hosts, block_rows, columns), "expert", split_axis=0, concat_axis=0, tiled=True
    )
    ordered = reorder(spread, old_host, new_host, [order])
    moved_weight = lax.all_to_all(ordered, "expert", split_axis=0, concat_axis=0, tiled=True)
    moved_weight = moved_weight.reshape(hidden_units, columns)
    rows, low, high, *part = first_parts(one, order)
    part = dict(zip(FIRST[1:] + SECOND, [*part, *second_parts(two, rows)]))

    gathered = lax.all_gather(moved_weight, ("ring", "near"), axis=0, tiled=False)
    up_sum, down_sum = low, high
    stacked = jnp.concatenate(
        [
            first_moment.reshape(hosts, block_rows, columns),
            second_moment.reshape(hosts, block_rows, columns),
        ],
        axis=1,
    )
    stacked, part[0] = lax.optimization_barrier((stacked, part[0]))
    spread = lax.all_to_all(stacked, "expert", split_axis=0, concat_axis=0, tiled=True)
    ordered = reorder(spread, old_host, new_host, [])
    moments = lax.all_to_all(ordered, "expert", split_axis=0, concat_axis=0, tiled=True)
    for step in range(1, N_FAR // 2 + 1):
        last = [up_sum, down_sum]
        up_sum = lax.ppermute(up_sum, "ring", UP)
        down_sum = lax.ppermute(down_sum, "ring", DOWN)
        if step < N_FAR // 2:
            up_part, down_part = part[N_FAR // 2 - step], part[step - N_FAR // 2]
            if step == 1:
                up_sum = jnp.concatenate([add(up_sum, up_part[:half]), up_part[half:]])
                down_sum = jnp.concatenate([down_part[:half], add(down_sum, down_part[half:])])
            else:
                up_sum, down_sum = add(up_sum, up_part), add(down_sum, down_part)
    far = lax.ppermute(produce(True, place, rows, gathered, last), "half", SWAP)
    near = produce(False, place, rows, gathered, [])
    output = assemble(place, near, far)
    new_weight, new_first, new_second = adam(moved_weight, moments, part[0], up_sum, down_sum, output)
    return (output[None], new_weight[None], new_first[None], new_second[None])


def solution(mesh):
    hosts = mesh.shape["expert"]
    grid = Mesh(mesh.devices.reshape(N_FAR, 2, 2, hosts), ("ring", "near", "half", "expert"))
    shards = P("expert", None, ("ring", "near", "half"))
    tokens = P("expert", ("ring", "near", "half"), None)
    return jax.shard_map(
        local,
        mesh=grid,
        in_specs=(shards, shards, shards, tokens, tokens, tokens, P(), P(), P()),
        out_specs=(tokens, shards, shards, shards),
        check_vma=False,
    )
```

```python
import functools

import jax
import jax.numpy as jnp
from jax import lax
from jax.experimental import pallas as pl
from jax.experimental.pallas import tpu as pltpu
from jax.sharding import Mesh, PartitionSpec as P

beta_one = 0.9
beta_two = 0.999
learning_rate = 0.001
epsilon_value = 1e-08
bias_one = 0.9999734386011124
bias_two = 0.0952078528863

N_FAR = 8
N_Z = 16
TEAM = ("near", "half")
SWAP = [(0, 1), (1, 0)]
UP = [(i, (i + 1) % N_FAR) for i in range(N_FAR)]
DOWN = [(i, (i - 1) % N_FAR) for i in range(N_FAR)]
VMEM = pl.BlockSpec(memory_space=pltpu.VMEM)
SMEM = pl.BlockSpec(memory_space=pltpu.SMEM)
ANY = pl.BlockSpec(memory_space=pl.ANY)
FIRST = [4, 3, -3]
SECOND = [2, -2, 1, -1, 0]


def shape(dims, dtype=jnp.bfloat16):
    return jax.ShapeDtypeStruct(dims, dtype)


def cost(flops, moved):
    return pl.CostEstimate(flops=flops, bytes_accessed=moved, transcendentals=0)


def prepare_kernel(place, new_host, counts, gate, up, cotangent, one, two):
    ring, member, host = place[0], place[1], place[2]
    expert = jnp.int32(0)
    for k in range(new_host.shape[0]):
        expert = jnp.where(new_host[k] == host, k, expert)
    live = counts[ring * 4 + member, expert]
    value = gate[...].astype(jnp.float32)
    activated = value / (1.0 + jnp.exp(-value)) * up[...].astype(jnp.float32)
    slot = lax.broadcasted_iota(jnp.int32, activated.shape, 0)
    hidden = jnp.where(slot < live, activated, 0.0).astype(one.dtype)
    for mate in range(4):
        for k in range(hidden.shape[1] // 128):
            one[mate, len(FIRST) + k] = hidden[:, k * 128 : (k + 1) * 128]
    for group, blocks in ((FIRST, one), (SECOND, two)):
        for i, distance in enumerate(group):
            owner = lax.rem(ring + (distance + N_FAR), N_FAR) * 4
            for mate in range(4):
                start = pl.multiple_of((owner + mate) * 128, 128)
                blocks[mate, i] = cotangent[:, pl.ds(start, 128)]


def prepare(place, new_host, counts, gate, up, cotangent):
    return pl.pallas_call(
        prepare_kernel,
        out_shape=[
            shape((4, len(FIRST) + gate.shape[1] // 128, gate.shape[0], 128)),
            shape((4, len(SECOND), gate.shape[0], 128)),
        ],
        in_specs=[SMEM] * 3 + [VMEM] * 3,
        out_specs=[VMEM] * 2,
        cost_estimate=cost(0, 3 << 20),
        name="prepare",
    )(place, new_host, counts, gate, up, cotangent)


def part_of(blocks, i, rows):
    block = jnp.concatenate([blocks[mate, i] for mate in range(4)], axis=0)
    total = lax.dot_general(
        block, rows[...], (((0,), (0,)), ((), ())), preferred_element_type=jnp.float32
    )
    return total.astype(rows.dtype)


def first_kernel(blocks, after, rows, low, high, *out):
    size = blocks.shape[2]
    for mate in range(4):
        for k in range(blocks.shape[1] - len(FIRST)):
            rows[pl.ds(mate * size, size), pl.ds(k * 128, 128)] = blocks[mate, len(FIRST) + k]
    total = part_of(blocks, 0, rows)
    half = total.shape[0] // 2
    low[...] = total[:half]
    high[...] = total[half:]
    for i, ref in enumerate(out):
        ref[...] = part_of(blocks, i + 1, rows)


def first_parts(blocks, after):
    columns, hidden_units = blocks.shape[3], (blocks.shape[1] - len(FIRST)) * 128
    return pl.pallas_call(
        first_kernel,
        out_shape=[shape((4 * blocks.shape[2], hidden_units))]
        + [shape((columns // 2, hidden_units))] * 2
        + [shape((columns, hidden_units))] * (len(FIRST) - 1),
        in_specs=[VMEM, ANY],
        out_specs=[VMEM] * (len(FIRST) + 2),
        cost_estimate=cost(1 << 28, 3 << 20),
        name="first_parts",
    )(blocks, after)


def second_kernel(blocks, rows, after, *out):
    for i, ref in enumerate(out):
        ref[...] = part_of(blocks, i, rows)


def second_parts(blocks, rows, after):
    return pl.pallas_call(
        second_kernel,
        out_shape=[shape((blocks.shape[3], rows.shape[1]))] * len(SECOND),
        in_specs=[VMEM] * 2 + [ANY],
        out_specs=[VMEM] * len(SECOND),
        cost_estimate=cost(1 << 29, 3 << 20),
        name="second_parts",
    )(blocks, rows, after)


def produce_kernel(mate, place, rows, blocks, *refs):
    out = refs[-1]
    member = place[1]
    if mate:
        member = member + 1 - 2 * lax.rem(member, 2)
    size = out.shape[1]
    mine = rows[pl.ds(pl.multiple_of(member * size, size), size), :]
    columns = blocks.shape[2]
    for i in range(0, blocks.shape[0], 2):
        pair = jnp.concatenate([blocks[i], blocks[i + 1]], axis=1)
        total = jnp.dot(mine, pair, preferred_element_type=jnp.float32).astype(out.dtype)
        out[i] = total[:, :columns]
        out[i + 1] = total[:, columns:]


def produce(mate, place, rows, blocks, after):
    count, hidden_units, columns = blocks.shape
    size, step = rows.shape[0] // 4, 4
    return pl.pallas_call(
        functools.partial(produce_kernel, mate),
        out_shape=shape((count, size, columns)),
        grid=(count // step,),
        in_specs=[
            SMEM,
            pl.BlockSpec(rows.shape, lambda i: (0, 0)),
            pl.BlockSpec((step, hidden_units, columns), lambda i: (i, 0, 0)),
        ]
        + [ANY] * len(after),
        out_specs=pl.BlockSpec((step, size, columns), lambda i: (i, 0, 0)),
        cost_estimate=cost(count << 25, 5 << 20),
        name="produce",
    )(place, rows, blocks, *after)


def reorder_kernel(old_host, new_host, value, *refs):
    out = refs[-1]
    for k in range(value.shape[0]):
        out[new_host[k]] = value[old_host[k]]


def reorder(value, old_host, new_host, after):
    return pl.pallas_call(
        reorder_kernel,
        out_shape=shape(value.shape, value.dtype),
        in_specs=[SMEM] * 2 + [VMEM] + [ANY] * len(after),
        out_specs=VMEM,
        cost_estimate=cost(0, 2 * value.size * value.dtype.itemsize),
        name="reorder",
    )(old_host, new_host, value, *after)


def assemble_kernel(place, near, far, out):
    half = lax.rem(place[1], 2)
    for owner in range(N_Z):
        for side, ref in ((half, near), (1 - half, far)):
            start = pl.multiple_of((2 * owner + side) * 128, 128)
            out[:, pl.ds(start, 128)] = ref[owner]


def assemble(place, near, far):
    return pl.pallas_call(
        assemble_kernel,
        out_shape=shape((near.shape[1], 2 * N_Z * 128)),
        in_specs=[SMEM] + [VMEM] * 2,
        out_specs=VMEM,
        cost_estimate=cost(0, 2 << 20),
        name="assemble",
    )(place, near, far)


def adam_kernel(weight, moments, part, rising, falling, after, new_weight, new_first, new_second):
    hosts, both, _ = moments.shape
    step = both // 2
    grad = part[...].astype(jnp.float32) + rising[...].astype(jnp.float32)
    grad = (grad + falling[...].astype(jnp.float32)).T
    for d in range(hosts):
        at = pl.ds(d * step, step)
        g = grad[d * step : (d + 1) * step]
        first = beta_one * moments[d, :step].astype(jnp.float32) + (1.0 - beta_one) * g
        second = beta_two * moments[d, step:].astype(jnp.float32) + (1.0 - beta_two) * g * g
        update = (
            learning_rate * (first / bias_one) / (jnp.sqrt(second / bias_two) + epsilon_value)
        )
        new_first[at] = first
        new_second[at] = second
        new_weight[at] = (weight[at].astype(jnp.float32) - update).astype(new_weight.dtype)


def adam(weight, moments, part, rising, falling, after):
    return pl.pallas_call(
        adam_kernel,
        out_shape=[
            shape(weight.shape),
            shape(weight.shape, jnp.float32),
            shape(weight.shape, jnp.float32),
        ],
        in_specs=[VMEM] * 5 + [ANY],
        out_specs=[VMEM] * 3,
        cost_estimate=cost(0, 3 << 20),
        name="adam",
    )(weight, moments, part, rising, falling, after)


def add(left, right):
    return (left.astype(jnp.float32) + right.astype(jnp.float32)).astype(jnp.bfloat16)


def local(
    weight, first_moment, second_moment, gate_act, up_act, out_grad, old_host, new_host, counts
):
    hosts = lax.axis_size("expert")
    ring, member = lax.axis_index("ring"), lax.axis_index(TEAM)
    at = jnp.arange(3, dtype=jnp.int32)
    place = jnp.where(at == 0, ring, jnp.where(at == 1, member, lax.axis_index("expert")))
    hidden_units, columns = weight.shape[1:]
    block_rows = hidden_units // hosts
    half = columns // 2

    one, two = prepare(place, new_host, counts, gate_act[0], up_act[0], out_grad[0])
    order = two
    spread = lax.all_to_all(
        weight.reshape(hosts, block_rows, columns), "expert", split_axis=0, concat_axis=0, tiled=True
    )
    ordered = reorder(spread, old_host, new_host, [order])
    moved_weight = lax.all_to_all(ordered, "expert", split_axis=0, concat_axis=0, tiled=True)
    moved_weight = moved_weight.reshape(hidden_units, columns)
    one, moved_weight = lax.optimization_barrier((one, moved_weight))
    one = lax.all_to_all(one, TEAM, split_axis=0, concat_axis=0, tiled=True)
    two = lax.all_to_all(two, TEAM, split_axis=0, concat_axis=0, tiled=True)
    rows, low, high, *part = first_parts(one, order)
    part = dict(zip(FIRST[1:], part))

    gathered = lax.all_gather(moved_weight, ("ring", "near"), axis=0, tiled=False)
    up_sum, down_sum = low, high
    for step in range(1, N_FAR // 2 + 1):
        if step == 3:
            last = [up_sum, down_sum]
        up_sum = lax.ppermute(up_sum, "ring", UP)
        down_sum = lax.ppermute(down_sum, "ring", DOWN)
        if step == 1:
            part |= zip(SECOND, second_parts(two, rows, up_sum))
            stacked = jnp.concatenate(
                [
                    first_moment.reshape(hosts, block_rows, columns),
                    second_moment.reshape(hosts, block_rows, columns),
                ],
                axis=1,
            ).astype(jnp.bfloat16)
            stacked, part[0] = lax.optimization_barrier((stacked, part[0]))
            spread = lax.all_to_all(stacked, "expert", split_axis=0, concat_axis=0, tiled=True)
            ordered = reorder(spread, old_host, new_host, [])
            moments = lax.all_to_all(ordered, "expert", split_axis=0, concat_axis=0, tiled=True)
        if step < N_FAR // 2:
            up_part, down_part = part[N_FAR // 2 - step], part[step - N_FAR // 2]
            if step == 1:
                up_sum = jnp.concatenate([add(up_sum, up_part[:half]), up_part[half:]])
                down_sum = jnp.concatenate([down_part[:half], add(down_sum, down_part[half:])])
            else:
                up_sum, down_sum = add(up_sum, up_part), add(down_sum, down_part)
    far = lax.ppermute(produce(True, place, rows, gathered, last), "half", SWAP)
    near = produce(False, place, rows, gathered, [])
    output = assemble(place, near, far)
    new_weight, new_first, new_second = adam(moved_weight, moments, part[0], up_sum, down_sum, output)
    return (output[None], new_weight[None], new_first[None], new_second[None])


def solution(mesh):
    hosts = mesh.shape["expert"]
    grid = Mesh(mesh.devices.reshape(N_FAR, 2, 2, hosts), ("ring", "near", "half", "expert"))
    shards = P("expert", None, ("ring", "near", "half"))
    tokens = P("expert", ("ring", "near", "half"), None)
    return jax.shard_map(
        local,
        mesh=grid,
        in_specs=(shards, shards, shards, tokens, tokens, tokens, P(), P(), P()),
        out_specs=(tokens, shards, shards, shards),
        check_vma=False,
    )
```
